32 devices in a mesh: dp: 4 (over z), expert: 4 (over y, core), loop: 2 (over x).
Axes of the slice: x: 2, y: 2, z: 4, core: 2. Of those that a mesh axis runs over, the one named last changes fastest.
Arguments:
- x_send: bfloat16 [512, 4096], P(('dp', 'expert', 'loop')), may hold values from -6 to 6
- cot_send: bfloat16 [512, 4096], P(('dp', 'expert', 'loop')), may hold values from -6 to 6
- counts: int32 [32, 4], P(('dp', 'expert', 'loop')), may hold values from 0 to 4, as said below
- w_gate: bfloat16 [4, 4096, 768], P('expert', None, 'loop'), may hold values from -0.09375 to 0.09375
- w_up: bfloat16 [4, 4096, 768], P('expert', None, 'loop'), may hold values from -0.09375 to 0.09375
- w_down: bfloat16 [4, 4096, 768], P('expert', None, 'loop'), may hold values from -0.21875 to 0.21875
Outputs:
- grad_rows: bfloat16 [512, 4096], P(('dp', 'expert', 'loop'))
- grad_down: float32 [4, 4096, 768], P('expert', 'dp', 'loop')
The draws below stay inside these ranges and needn't reach their ends.
Inputs may be any that keep to these rules, and one draw needn't show every extreme that they name: counts[s, e] is how many of the 4 slots of device s for owner e hold rows, filled from slot 0; in each group of 8 consecutive devices one owner, drawn anew, receives 4 rows from every device, and every other owner at most 2 from each device.
All inputs are finite; a program needn't handle non-finite values.
Results may differ from the reference program's by a relative error of at most 0.0095.
Values may be sent and summed in bfloat16 or wider, within the bound.
No kernel may reach another device: no remote copies, remote signals or barrier semaphores. Data moves between devices by JAX's collectives and lax.ppermute only.
A program may use at most 64 MiB of HBM per device.

```python
import jax
import jax.numpy as jnp
from jax import lax

D = 4096
HID = 768
C = 4
SOURCES = 32
N_DP = 4
N_EXPERT = 4
N_LOOP = 2


def draw_counts(key, part):
    base_key = jax.random.fold_in(key, 17)
    first_key, second_key = jax.random.split(base_key)
    base = jax.random.randint(first_key, (N_DP, N_EXPERT * N_LOOP, N_EXPERT), 0, C // 2 + 1)
    busiest = jax.random.randint(second_key, (N_DP,), 0, N_EXPERT)
    is_busiest = jnp.arange(N_EXPERT)[None, :] == busiest[:, None]
    filled = jnp.where(is_busiest[:, None, :], C, base)
    return filled.reshape(N_DP * N_EXPERT * N_LOOP, N_EXPERT).astype(jnp.int32)


def with_spikes(result, own_key, source, target, shards_of, factor):
    def block_of(position):
        return (jnp.arange(result.shape[position]) // (result.shape[position] // shards_of)).reshape((-1,) + (1,) * (result.ndim - 1 - position))

    near = jax.random.permutation(own_key, shards_of)[block_of(target)]
    other_side = (block_of(target) + shards_of // 2) % shards_of
    return jnp.where((block_of(source) == near) | (block_of(source) == other_side), factor * result, result)


def block_scale(stream_key, dims, pieces, low, largest):
    factor_of = 1.0
    for dim, parts in pieces:
        draws = jax.random.uniform(jax.random.fold_in(jax.random.fold_in(stream_key, 6), dim), (parts,), jnp.float32, low / len(pieces), largest / len(pieces))
        factor_of = factor_of * jnp.repeat(jnp.exp(draws), dims[dim] // parts).reshape((-1,) + (1,) * (len(dims) - 1 - dim))
    return factor_of


def scatter_about(key, extent, width, reach, cuts=(), held_as=jnp.bfloat16):
    result = width * jax.random.normal(key, extent, jnp.float32)
    if cuts:
        result = result * block_scale(key, extent, cuts, -0.22, 0.18)
    return jnp.clip(result, -reach, reach).astype(held_as)


def heavy_noise(own_key, shape, spread, reach, cuts, heavy, kind=jnp.bfloat16):
    values = spread * jax.random.normal(own_key, shape, jnp.float32)
    if cuts:
        values = values * block_scale(own_key, shape, cuts, -0.22, 0.18)
    return jnp.clip(with_spikes(values, jax.random.fold_in(own_key, 3), *heavy), -reach, reach).astype(kind)


def setup_inputs(seed: int = 0) -> dict:
    key_of = jax.random.split(jax.random.key(seed), 7)
    x_send = scatter_about(key_of[0], (SOURCES * N_EXPERT * C, D), 1.0, 6.0, ((0, 32),))
    cot_send = heavy_noise(key_of[1], (SOURCES * N_EXPERT * C, D), 1.0, 6.0, ((0, 32),), (0, 1, 32, 2.75))
    counts = draw_counts(jax.random.fold_in(key_of[6], 71), 0)
    w_gate = scatter_about(key_of[3], (N_EXPERT, D, HID), D ** -0.5, 0.09375, ((0, 4), (2, 2)))
    w_up = scatter_about(key_of[4], (N_EXPERT, D, HID), D ** -0.5, 0.09375, ((0, 4), (2, 2)))
    w_down = scatter_about(key_of[5], (N_EXPERT, D, HID), HID ** -0.5, 0.21875, ((0, 4), (2, 2)))
    return dict(x_send=x_send, cot_send=cot_send, counts=counts, w_gate=w_gate, w_up=w_up, w_down=w_down)


def one_owner(bundle):
    rows_in, cot_in, gate_mat, up_mat, down_mat = bundle
    gate_pre = jnp.dot(rows_in, gate_mat, preferred_element_type=jnp.float32)
    up_proj = jnp.dot(rows_in, up_mat, preferred_element_type=jnp.float32)
    sigmoid_gate = jax.nn.sigmoid(gate_pre)
    active = gate_pre * sigmoid_gate
    hidden = (active * up_proj).astype(jnp.bfloat16)
    grad_hidden = jnp.dot(cot_in, down_mat, preferred_element_type=jnp.float32)
    grad_gate = (grad_hidden * up_proj * sigmoid_gate * (1.0 + gate_pre * (1.0 - sigmoid_gate))).astype(jnp.bfloat16)
    grad_upp = (grad_hidden * active).astype(jnp.bfloat16)
    block = HID // N_LOOP
    row_total = rows_in.shape[0]
    gate_blocks = grad_gate.astype(jnp.float32).reshape(row_total, N_LOOP, block)
    upp_blocks = grad_upp.astype(jnp.float32).reshape(row_total, N_LOOP, block)
    gate_table = gate_mat.astype(jnp.float32).reshape(D, N_LOOP, block)
    upp_table = up_mat.astype(jnp.float32).reshape(D, N_LOOP, block)
    partial_value = jnp.einsum("rbk,dbk->brd", gate_blocks, gate_table) + jnp.einsum("rbk,dbk->brd", upp_blocks, upp_table)
    rounded = lax.optimization_barrier(partial_value.astype(jnp.bfloat16))
    grad_input = jnp.sum(rounded.astype(jnp.float32), axis=0).astype(jnp.bfloat16)
    grad_weight = jnp.dot(cot_in.T, hidden, preferred_element_type=jnp.float32)
    return grad_input, grad_weight


def reference(x_send, cot_send, counts, w_gate, w_up, w_down):
    sources = N_DP * N_EXPERT * N_LOOP
    live_slot = jnp.arange(C, dtype=jnp.int32)[None, None, :] < counts[:, :, None]
    zero_value = jnp.zeros((), jnp.bfloat16)
    rows_three = x_send.reshape(sources, N_EXPERT, C, D)
    cots_three = cot_send.reshape(sources, N_EXPERT, C, D)
    rows_masked = jnp.where(live_slot[..., None], rows_three, zero_value)
    cots_masked = jnp.where(live_slot[..., None], cots_three, zero_value)
    rows_owner = rows_masked.reshape(N_DP, N_EXPERT, N_LOOP, N_EXPERT, C, D).transpose(3, 0, 1, 2, 4, 5).reshape(N_EXPERT, -1, D)
    cots_owner = cots_masked.reshape(N_DP, N_EXPERT, N_LOOP, N_EXPERT, C, D).transpose(3, 0, 1, 2, 4, 5).reshape(N_EXPERT, -1, D)
    grad_owner, grad_down = lax.map(one_owner, (rows_owner, cots_owner, w_gate, w_up, w_down))
    grad_rows = grad_owner.reshape(N_EXPERT, N_DP, N_EXPERT, N_LOOP, C, D).transpose(1, 2, 3, 0, 4, 5).reshape(-1, D)
    return grad_rows, grad_down
```

```python
import functools

import jax
import jax.numpy as jnp
from jax import lax
from jax.sharding import PartitionSpec as P

MOST_PEERS = 16


def by_groups(x_send, cot_send, counts, w_gate, w_up, w_down):
    owner_count = counts.shape[1]
    capacity = x_send.shape[0] // owner_count
    live_slot = (jnp.arange(capacity, dtype=jnp.int32)[None, :] < counts[0][:, None]).reshape(
        owner_count * capacity, 1
    )
    zero_value = jnp.zeros((), jnp.bfloat16)
    inputs = jnp.where(live_slot, x_send, zero_value)
    cotans = jnp.where(live_slot, cot_send, zero_value)
    arrived, arrived_cot = (
        lax.all_to_all(inputs, "expert", split_axis=0, concat_axis=0, tiled=True),
        lax.all_to_all(cotans, "expert", split_axis=0, concat_axis=0, tiled=True),
    )
    gathered, gathered_cot = (
        lax.all_gather(arrived, "loop", axis=0, tiled=True),
        lax.all_gather(arrived_cot, "loop", axis=0, tiled=True),
    )
    gate_local = w_gate[0]
    up_local = w_up[0]
    down_local = w_down[0]
    gate_pre = jnp.dot(gathered, gate_local, preferred_element_type=jnp.float32)
    up_proj = jnp.dot(gathered, up_local, preferred_element_type=jnp.float32)
    sigmoid_gate = jax.nn.sigmoid(gate_pre)
    active = gate_pre * sigmoid_gate
    hidden = (active * up_proj).astype(jnp.bfloat16)
    grad_hidden = jnp.dot(gathered_cot, down_local, preferred_element_type=jnp.float32)
    grad_gate = (
        grad_hidden * up_proj * sigmoid_gate * (1.0 + gate_pre * (1.0 - sigmoid_gate))
    ).astype(jnp.bfloat16)
    grad_upp = (grad_hidden * active).astype(jnp.bfloat16)
    contract_last = (((1,), (1,)), ((), ()))
    contract_first = (((0,), (0,)), ((), ()))
    partial_value = lax.dot_general(
        grad_gate, gate_local, contract_last, preferred_element_type=jnp.float32
    )
    partial_value = partial_value + lax.dot_general(
        grad_upp, up_local, contract_last, preferred_element_type=jnp.float32
    )
    summed = lax.psum_scatter(
        lax.optimization_barrier(partial_value.astype(jnp.bfloat16))
        .astype(jnp.float32)
        .astype(jnp.bfloat16),
        "loop",
        scatter_dimension=0,
        tiled=True,
    )
    grad_rows = lax.all_to_all(summed, "expert", split_axis=0, concat_axis=0, tiled=True)
    column_part = lax.all_to_all(gathered_cot, "dp", split_axis=1, concat_axis=0, tiled=True)
    hidden_all = lax.all_gather(hidden, "dp", axis=0, tiled=True)
    result = lax.dot_general(
        column_part, hidden_all, contract_first, preferred_element_type=jnp.float32
    )
    grad_down = result[None]
    return (grad_rows, grad_down)


def local(n_dp, n_expert, n_loop, x_send, cot_send, counts, w_gate, w_up, w_down):
    bf16, f32 = jnp.bfloat16, jnp.float32
    pair = 2 if n_expert % 2 == 0 else 1
    high = n_expert // pair
    rows, width = x_send.shape
    capacity = rows // n_expert
    e, l, d = lax.axis_index("expert"), lax.axis_index("loop"), lax.axis_index("dp")
    h, c = e // pair, e % pair

    def take(a, i):
        return lax.dynamic_index_in_dim(a, i, 0, keepdims=False)

    def swap_core(a):
        return lax.ppermute(a, "expert", [(i, i ^ 1) for i in range(n_expert)])

    def to_chip(a, kh, kl):
        def other(i):
            return ((i // n_loop) ^ (kh * pair)) * n_loop + ((i % n_loop) ^ kl)

        return lax.ppermute(
            a, ("expert", "loop"), [(i, other(i)) for i in range(n_expert * n_loop)]
        )

    def to_dp(a, k):
        return lax.ppermute(a, "dp", [(i, i ^ k) for i in range(n_dp)])

    live = (jnp.arange(capacity, dtype=jnp.int32)[None, :] < counts[0][:, None]).reshape(rows, 1)
    zero = jnp.zeros((), bf16)
    xm = jnp.where(live, x_send, zero).reshape(high, pair, capacity, width)
    cm = jnp.where(live, cot_send, zero).reshape(high, pair, capacity, width)
    both = jnp.stack([xm, cm], axis=1)
    keep = lax.dynamic_index_in_dim(both, c, 2, keepdims=True)
    if pair == 2:
        got = swap_core(lax.dynamic_index_in_dim(both, 1 - c, 2, keepdims=True))
        merged = jnp.concatenate([keep, got], axis=2)
    else:
        merged = keep
    merged = merged.reshape(high, 2 * pair * capacity, width)
    offsets = [(kh, kl) for kh in range(high) for kl in range(n_loop)]
    blocks = []
    for kh, kl in offsets:
        part = take(merged, h ^ kh)
        blocks.append(part if (kh, kl) == (0, 0) else to_chip(part, kh, kl))
    half = pair * capacity
    gathered = jnp.concatenate([b[:half] for b in blocks], axis=0)
    gathered_cot = jnp.concatenate([b[half:] for b in blocks], axis=0)

    gate_local, up_local, down_local = w_gate[0], w_up[0], w_down[0]
    gate_pre = jnp.dot(gathered, gate_local, preferred_element_type=f32)
    up_proj = jnp.dot(gathered, up_local, preferred_element_type=f32)
    sigmoid_gate = jax.nn.sigmoid(gate_pre)
    active = gate_pre * sigmoid_gate
    hidden = (active * up_proj).astype(bf16)
    grad_hidden = jnp.dot(gathered_cot, down_local, preferred_element_type=f32)
    grad_gate = (
        grad_hidden * up_proj * sigmoid_gate * (1.0 + gate_pre * (1.0 - sigmoid_gate))
    ).astype(bf16)
    grad_upp = (grad_hidden * active).astype(bf16)
    contract_last = (((1,), (1,)), ((), ()))
    contract_first = (((0,), (0,)), ((), ()))
    partial_value = lax.dot_general(
        grad_gate, gate_local, contract_last, preferred_element_type=f32
    )
    partial_value = partial_value + lax.dot_general(
        grad_upp, up_local, contract_last, preferred_element_type=f32
    )
    part_b = lax.optimization_barrier(partial_value.astype(bf16))

    slices = width // n_dp
    cots, hids = [], []
    for k in range(n_dp):
        cols = lax.dynamic_slice_in_dim(gathered_cot, (d ^ k) * slices, slices, 1)
        if k:
            sent = to_dp(jnp.concatenate([cols, hidden], axis=1), k)
            cots.append(sent[:, :slices])
            hids.append(sent[:, slices:])
        else:
            cots.append(cols)
            hids.append(hidden)

    sums = []
    for kh in range(high):
        total = None
        for kl in range(n_loop):
            i = kh * n_loop + kl
            part = part_b[i * half : (i + 1) * half]
            if (kh, kl) != (0, 0):
                part = to_chip(part, kh, kl)
            part = part.astype(f32)
            total = part if total is None else total + part
        sums.append(total.astype(bf16))
    done = jnp.stack(sums).reshape(high, pair, capacity, width)
    if pair == 2:
        back = swap_core(done[:, 1])
        mine = done[:, 0]
        low = jnp.where(c == 0, mine, back)
        upp = jnp.where(c == 0, back, mine)
        done = jnp.stack([low, upp], axis=1)
    owner = jnp.stack([take(done, h ^ k) for k in range(high)])
    grad_rows = owner.reshape(rows, width)

    result = lax.dot_general(
        jnp.concatenate(cots, axis=0),
        jnp.concatenate(hids, axis=0),
        contract_first,
        preferred_element_type=f32,
    )
    return (grad_rows, result[None])


def solution(mesh):
    in_specs = (
        P(("dp", "expert", "loop"), None),
        P(("dp", "expert", "loop"), None),
        P(("dp", "expert", "loop"), None),
        P("expert", None, "loop"),
        P("expert", None, "loop"),
        P("expert", None, "loop"),
    )
    out_specs = (P(("dp", "expert", "loop"), None), P("expert", "dp", "loop"))
    n_dp, n_expert, n_loop = (mesh.shape[a] for a in ("dp", "expert", "loop"))
    sizes_fit = all(n & (n - 1) == 0 for n in (n_dp, n_expert, n_loop))
    if sizes_fit and n_dp + n_expert * n_loop <= MOST_PEERS:
        body = functools.partial(local, n_dp, n_expert, n_loop)
    else:
        body = by_groups
    return jax.shard_map(body, mesh=mesh, in_specs=in_specs, out_specs=out_specs, check_vma=False)
```
